32 devices in a mesh: dp: 4 (over y, x), seq: 8 (over z, core).
Axes of the slice: x: 2, y: 2, z: 4, core: 2. Of those that a mesh axis runs over, the one named last changes fastest.
Arguments:
- tiles: bfloat16 [4, 8192, 768], P('dp', 'seq'), may hold values from -48 to 48
- tile_count: int32 [4], P('dp'), may hold values from 4097 to 8192
- offsets: int32 [16], replicated, may hold values from 0 to 15
- w_query: bfloat16 [768, 768], replicated, may hold values from -0.375 to 0.375
- w_key: bfloat16 [768, 768], replicated, may hold values from -0.375 to 0.375
- w_value: bfloat16 [768, 768], replicated, may hold values from -0.21875 to 0.21875
- w_out: bfloat16 [768, 768], replicated, may hold values from -0.21875 to 0.21875
- cotangent: bfloat16 [4, 8192, 768], P('dp', 'seq'), may hold values from -0.046875 to 0.046875
Outputs:
- branch: bfloat16 [4, 8192, 768], P('dp', 'seq')
- grad_out: float32 [768, 768], P(None, 'seq')
The draws below stay inside these ranges and needn't reach their ends.
All inputs are finite; a program needn't handle non-finite values.
Results may differ from the reference program's by a relative error of at most 0.0095.
The reference program's roundings to bfloat16 on the way count: a program that leaves them out, or rounds other values in their place, can miss the bound.
Values may be sent and summed in bfloat16 or wider, within the bound.
A program may use at most 128 MiB of HBM per device.

```python
import jax
import jax.numpy as jnp
from jax import lax

D = 768
ATTENTION_HEADS = 16
HEAD_SIZE = 48
SEG = 1024
RATE = 16
SLIDES = 4
TOKENS = 8192


def draw_tiles(key, part):
    extent = (SLIDES, TOKENS, D)
    normal_key = jax.random.fold_in(key, 0)
    values = jax.random.truncated_normal(normal_key, -6.0, 6.0, extent, jnp.float32)
    return values.astype(jnp.bfloat16)


def plant(entries, key, least, high):
    longest = entries.shape.index(max(entries.shape))
    spots = []
    for shift in (0, 1):
        where = [jax.random.randint(jax.random.fold_in(key, axis), (), 0, length) for axis, length in enumerate(entries.shape)]
        where[longest] = (where[longest] + shift) % entries.shape[longest]
        spots.append(tuple(where))
    return entries.at[spots[0]].set(least).at[spots[1]].set(high)


def raised(drawn, key, source, target, parts, factor):
    def block_of(dim):
        return (jnp.arange(drawn.shape[dim]) // (drawn.shape[dim] // parts)).reshape((-1,) + (1,) * (drawn.ndim - 1 - dim))

    first = jax.random.permutation(key, parts)[block_of(target)]
    other_side = (block_of(target) + parts // 2) % parts
    return jnp.where((block_of(source) == first) | (block_of(source) == other_side), factor * drawn, drawn)


def block_scale(key, shape, shards, low, top_value):
    def one(dim, parts):
        draws = jax.random.uniform(jax.random.fold_in(jax.random.fold_in(key, 6), dim), (parts,), jnp.float32, low / len(shards), top_value / len(shards))
        return jnp.repeat(jnp.exp(draws), shape[dim] // parts).reshape((-1,) + (1,) * (len(shape) - dim - 1))

    factor_of = one(*shards[0])
    for cut in shards[1:]:
        factor_of = factor_of * one(*cut)
    return factor_of


def bell_draw(own_key, dims, scale, limit, pieces=(), held_as=jnp.bfloat16):
    array = jax.random.normal(own_key, dims, jnp.float32) * scale
    if len(pieces) > 0:
        array = block_scale(own_key, dims, pieces, -0.22, 0.18) * array
    return jnp.clip(array, min=-limit, max=limit).astype(held_as)


def gaussian_with(key, shape, scale, bound, pieces, heavy, kind=jnp.bfloat16):
    array = scale * jax.random.normal(key, shape, jnp.float32)
    if pieces:
        array = array * block_scale(key, shape, pieces, -0.22, 0.18)
    return jnp.clip(raised(array, jax.random.fold_in(key, 3), *heavy), -bound, bound).astype(kind)


def setup_inputs(seed: int = 0) -> dict:
    arg_keys = jax.random.split(jax.random.key(seed), 9)
    return {
        "tiles": draw_tiles(jax.random.fold_in(arg_keys[8], 71), 0),
        "tile_count": plant(jax.random.randint(arg_keys[1], (SLIDES,), TOKENS // 2 + 1, TOKENS + 1), jax.random.fold_in(arg_keys[1], 1), TOKENS // 2 + 1, TOKENS).astype(jnp.int32),
        "offsets": plant(jax.random.randint(arg_keys[2], (ATTENTION_HEADS,), 0, RATE), jax.random.fold_in(arg_keys[2], 1), 0, RATE - 1).astype(jnp.int32),
        "w_query": bell_draw(arg_keys[3], (D, D), (D // 3) ** -0.5, 0.375),
        "w_key": bell_draw(arg_keys[4], (D, D), (D // 3) ** -0.5, 0.375),
        "w_value": bell_draw(arg_keys[5], (D, D), D ** -0.5, 0.21875),
        "w_out": bell_draw(arg_keys[6], (D, D), D ** -0.5, 0.21875),
        "cotangent": gaussian_with(arg_keys[7], (SLIDES, TOKENS, D), (TOKENS * SLIDES) ** -0.5, 0.046875, ((0, 4), (1, 8)), (1, 2, 8, 2.0)),
    }


NEGATIVE_FLOOR = -1e30


def project(inputs, weight):
    return jnp.dot(inputs, weight, preferred_element_type=jnp.float32).astype(jnp.bfloat16)


def select_rows(tensor, offsets):
    segment_height = tensor.shape[0]
    grouped = tensor.reshape(segment_height // RATE, RATE, ATTENTION_HEADS, HEAD_SIZE).astype(jnp.float32)
    onehot = (jnp.arange(RATE, dtype=jnp.int32)[:, None] == offsets[None, :]).astype(jnp.float32)
    return jnp.einsum('arhd,rh->ahd', grouped, onehot).astype(jnp.bfloat16)


def segment_attention(blocks):
    query_seg, key_seg, value_seg, alive_seg = blocks
    scores = jnp.einsum('qhd,khd->hqk', query_seg.astype(jnp.float32), key_seg.astype(jnp.float32)) * (HEAD_SIZE ** -0.5)
    scores = jnp.where(alive_seg[None, None, :], scores, NEGATIVE_FLOOR)
    maxima = jnp.max(scores, axis=-1)
    weights = jnp.exp(scores - maxima[..., None])
    totals = jnp.sum(weights, axis=-1)
    rounded = lax.optimization_barrier(weights.astype(jnp.bfloat16))
    weighted = jnp.einsum('hqk,khd->qhd', rounded.astype(jnp.float32), value_seg.astype(jnp.float32))
    return maxima.T, totals.T, weighted


def combine(local, dilated_branch, offsets, is_live):
    local_max, local_total, local_sum = local
    dilated_row_max, dilated_value_total, dilated_row_sum = dilated_branch
    segment_height = local_max.shape[0]
    dilation_match = jnp.arange(RATE, dtype=jnp.int32)[:, None] == offsets[None, :]
    dense_row_max = jnp.where(dilation_match[None], dilated_row_max[:, None, :], NEGATIVE_FLOOR).reshape(segment_height, ATTENTION_HEADS)
    dense_value_total = jnp.where(dilation_match[None], dilated_value_total[:, None, :], 0.0).reshape(segment_height, ATTENTION_HEADS)
    dense_row_sum = jnp.where(dilation_match[None, :, :, None], dilated_row_sum[:, None], 0.0).reshape(segment_height, ATTENTION_HEADS, HEAD_SIZE)
    top = jnp.maximum(local_max, dense_row_max)
    near = jnp.exp(local_max - top)
    far = jnp.exp(dense_row_max - top)
    attn = (near[..., None] * local_sum + far[..., None] * dense_row_sum) / (near * local_total + far * dense_value_total)[..., None]
    attn = jnp.where(is_live[:, None, None], attn, 0.0)
    return attn.reshape(segment_height, D).astype(jnp.bfloat16)


def reference(tiles, tile_count, offsets, w_query, w_key, w_value, w_out, cotangent):
    outputs = []
    gradient = jnp.zeros((D, D), jnp.float32)
    segments = TOKENS // SEG
    picked = TOKENS // RATE
    for slide in range(SLIDES):
        inputs = tiles[slide]
        live_count = tile_count[slide]
        query_proj = project(inputs, w_query).reshape(TOKENS, ATTENTION_HEADS, HEAD_SIZE)
        key_proj = project(inputs, w_key).reshape(TOKENS, ATTENTION_HEADS, HEAD_SIZE)
        value_proj = project(inputs, w_value).reshape(TOKENS, ATTENTION_HEADS, HEAD_SIZE)
        is_live = jnp.arange(TOKENS, dtype=jnp.int32) < live_count
        local = lax.map(segment_attention, (query_proj.reshape(segments, SEG, ATTENTION_HEADS, HEAD_SIZE), key_proj.reshape(segments, SEG, ATTENTION_HEADS, HEAD_SIZE), value_proj.reshape(segments, SEG, ATTENTION_HEADS, HEAD_SIZE), is_live.reshape(segments, SEG)))
        local = (local[0].reshape(TOKENS, ATTENTION_HEADS), local[1].reshape(TOKENS, ATTENTION_HEADS), local[2].reshape(TOKENS, ATTENTION_HEADS, HEAD_SIZE))
        query_sel = select_rows(query_proj, offsets).transpose(1, 0, 2)
        key_sel = select_rows(key_proj, offsets).transpose(1, 0, 2)
        value_sel = select_rows(value_proj, offsets).transpose(1, 0, 2)

        def head_attention(blocks):
            query_head, key_head, value_head, offset = blocks
            key_live = jnp.arange(picked, dtype=jnp.int32) * RATE + offset < live_count
            scores = jnp.dot(query_head, key_head.T, preferred_element_type=jnp.float32) * (HEAD_SIZE ** -0.5)
            scores = jnp.where(key_live[None, :], scores, NEGATIVE_FLOOR)
            maxima = jnp.max(scores, axis=-1)
            weights = jnp.exp(scores - maxima[:, None])
            totals = jnp.sum(weights, axis=-1)
            weighted = jnp.dot(weights.astype(jnp.bfloat16), value_head, preferred_element_type=jnp.float32)
            return maxima, totals, weighted

        dilated_branch = lax.map(head_attention, (query_sel, key_sel, value_sel, offsets))
        dilated_branch = (dilated_branch[0].T, dilated_branch[1].T, dilated_branch[2].transpose(1, 0, 2))
        attn = combine(local, dilated_branch, offsets, is_live)
        outputs.append(jnp.dot(attn, w_out, preferred_element_type=jnp.float32).astype(jnp.bfloat16))
        gradient = gradient + jnp.dot(attn.T, cotangent[slide], preferred_element_type=jnp.float32)
    return jnp.stack(outputs), gradient
```

```python
import functools

import jax
import jax.numpy as jnp
from jax import lax
from jax.experimental import pallas as pl
from jax.experimental.pallas import tpu as pltpu
from jax.sharding import PartitionSpec as P

ATTENTION_HEADS = 16
HEAD_SIZE = 48
SEG = 1024
RATE = 16
NEGATIVE_FLOOR = -1e30
LOG2_SCALE = 1.4426950408889634 / HEAD_SIZE**0.5
PAD = 16
BF16 = jnp.bfloat16
F32 = jnp.float32
VMEM = pl.BlockSpec(memory_space=pltpu.VMEM)
SMEM = pl.BlockSpec(memory_space=pltpu.SMEM)


def dot(a, b, ca=1, cb=0):
    return lax.dot_general(a, b, (((ca,), (cb,)), ((), ())), preferred_element_type=F32)


def head_rows(head):
    return pl.ds(pl.multiple_of(head * HEAD_SIZE, PAD), HEAD_SIZE)


def scaled_query(query):
    scaled = query.astype(F32) * LOG2_SCALE
    high = scaled.astype(BF16)
    low = (scaled - high.astype(F32)).astype(BF16)
    return jnp.concatenate([high, low, jnp.ones((PAD, query.shape[1]), BF16)], 0)


def masked_key(key, dead):
    row = lax.broadcasted_iota(jnp.int32, (PAD, key.shape[1]), 0)
    mask = jnp.where(dead & (row == 0), NEGATIVE_FLOOR, 0.0).astype(BF16)
    return jnp.concatenate([key, key, mask], 0)


def counted_value(value):
    return jnp.concatenate([value, jnp.ones((PAD, value.shape[1]), BF16)], 0)


def lanes(width):
    return lax.broadcasted_iota(jnp.int32, (PAD, width), 1)


def selector(length, offset):
    shape = (length, length // RATE)
    token = lax.broadcasted_iota(jnp.int32, shape, 0)
    pick = lax.broadcasted_iota(jnp.int32, shape, 1)
    return jnp.where(token == RATE * pick + offset, 1.0, 0.0).astype(BF16)


def project_kernel(offsets, x, wq, wk, wv, q_out, k_out, v_out, sel_out):
    length = x.shape[0]
    picked = length // RATE
    tiles = x[...]
    for weight, out in ((wk, k_out), (wv, v_out), (wq, q_out)):
        out[...] = dot(weight[...].T, tiles, 1, 1).astype(BF16)

    def pick(head, carry):
        rows = head_rows(head)
        onehot = selector(length, offsets[head])
        both = jnp.concatenate([k_out[rows, :], v_out[rows, :]], 0)
        chosen = dot(both, onehot).astype(BF16)
        sel_out[rows, :picked] = chosen[:HEAD_SIZE]
        sel_out[rows, picked:] = chosen[HEAD_SIZE:]
        return carry

    lax.fori_loop(0, ATTENTION_HEADS, pick, 0, unroll=4)


def local_kernel(base, live, q, k, v, out):
    length = q.shape[1]
    chunk = length // 2
    parts = 4
    step = length // parts
    dead = lanes(length) + base[0] >= live[0]

    def one_head(head, carry):
        rows = head_rows(head)
        query = scaled_query(q[rows, :])
        key = masked_key(k[rows, :], dead).T
        value = counted_value(v[rows, :])
        scores = dot(key, query[:, :chunk])
        for index in range(length // chunk):
            here = scores
            if (index + 1) * chunk < length:
                scores = dot(key, query[:, (index + 1) * chunk : (index + 2) * chunk])
            peak = jnp.max(here, axis=0, keepdims=True)
            total = None
            for part in range(parts):
                cut = slice(part * step, (part + 1) * step)
                weights = jnp.exp2(here[cut] - peak).astype(BF16)
                piece = dot(value[:, cut], weights)
                total = piece if total is None else total + piece
            done = total[:HEAD_SIZE] / total[HEAD_SIZE : HEAD_SIZE + 1]
            out[rows, index * chunk : (index + 1) * chunk] = done.astype(BF16)
        return carry

    lax.fori_loop(0, ATTENTION_HEADS, one_head, 0)


def dilated_kernel(base, live, offsets, q, k, v, gathered, near, w_out, cot, branch, grad, attn):
    length = q.shape[1]
    picked = length // RATE
    shards = gathered.shape[0]
    width = 2 * picked
    position = lanes(length) + base[0]
    dead = position >= live[0]
    slot = lanes(shards * width)
    inside = slot % width
    key_position = slot // width * length + inside * RATE

    def attend(key, query, value):
        scores = dot(key, query, 0, 0)
        peak = jnp.max(scores, axis=0, keepdims=True)
        weights = jnp.exp2(scores - peak).astype(BF16)
        return peak, dot(value, weights)

    def one_head(head, carry):
        rows = head_rows(head)
        offset = offsets[head]
        onehot = selector(length, offset)
        query = dot(scaled_query(q[rows, :]), onehot).astype(BF16)
        local_max, local_sum = attend(masked_key(k[rows, :], dead), query, counted_value(v[rows, :]))
        both = jnp.concatenate([gathered[shard, rows, :] for shard in range(shards)], 1)
        key_dead = (inside >= picked) | (key_position + offset >= live[0])
        value = jnp.concatenate([both[:, picked:], both[:, :picked]], 1)
        far_max, far_sum = attend(masked_key(both, key_dead), query, counted_value(value))
        top = jnp.maximum(local_max, far_max)
        total = jnp.exp2(local_max - top) * local_sum + jnp.exp2(far_max - top) * far_sum
        chosen = (total[:HEAD_SIZE] / total[HEAD_SIZE : HEAD_SIZE + 1]).astype(BF16)
        spread = dot(chosen, onehot, 1, 1)
        is_picked = position[:1] % RATE == offset
        merged = jnp.where(is_picked, spread, near[rows, :].astype(F32))
        attn[rows, :] = jnp.where(dead[:1], 0.0, merged).astype(BF16)
        return carry

    lax.fori_loop(0, ATTENTION_HEADS, one_head, 0, unroll=2)
    grad[...] = dot(attn[...], cot[...]).astype(BF16).T
    branch[...] = dot(attn[...].T, w_out[...]).astype(BF16)


def params():
    return pltpu.CompilerParams(vmem_limit_bytes=60 << 20)


def body(tiles, tile_count, offsets, w_query, w_key, w_value, w_out, cotangent):
    inputs = tiles[0]
    length, width = inputs.shape
    assert length == SEG
    picked = length // RATE
    base = (lax.axis_index("seq") * length).astype(jnp.int32).reshape(1)
    half = jax.ShapeDtypeStruct((width, length), BF16)
    query, key, value, chosen = pl.pallas_call(
        project_kernel,
        out_shape=(half, half, half, jax.ShapeDtypeStruct((width, 2 * picked), BF16)),
        in_specs=[SMEM] + [VMEM] * 4,
        out_specs=(VMEM,) * 4,
        compiler_params=params(),
    )(offsets, inputs, w_query, w_key, w_value)
    gathered = lax.all_gather(chosen, "seq", axis=0)
    near = pl.pallas_call(
        local_kernel,
        out_shape=half,
        in_specs=[SMEM] * 2 + [VMEM] * 3,
        out_specs=VMEM,
        compiler_params=params(),
        cost_estimate=pl.CostEstimate(flops=2 * 10**10, bytes_accessed=6 * 10**6, transcendentals=2 * 10**7),
    )(base, tile_count, query, key, value)
    branch, grad = pl.pallas_call(
        dilated_kernel,
        out_shape=(
            jax.ShapeDtypeStruct((length, width), BF16),
            jax.ShapeDtypeStruct((width, width), BF16),
        ),
        in_specs=[SMEM] * 3 + [VMEM] * 7,
        out_specs=(VMEM,) * 2,
        scratch_shapes=[pltpu.VMEM((width, length), BF16)],
        compiler_params=params(),
    )(base, tile_count, offsets, query, key, value, gathered, near, w_out, cotangent[0])
    share = lax.psum_scatter(grad, "seq", scatter_dimension=0, tiled=True)
    grad_part = lax.psum(share, "dp").astype(F32).T
    return (branch[None], grad_part)


def solution(mesh):
    in_specs = (P("dp", "seq", None), P("dp"), P(), P(), P(), P(), P(), P("dp", "seq", None))
    out_specs = (P("dp", "seq", None), P(None, "seq"))
    return jax.shard_map(body, mesh=mesh, in_specs=in_specs, out_specs=out_specs, check_vma=False)
```

```python
import functools

import jax
import jax.numpy as jnp
from jax import lax
from jax.experimental import pallas as pl
from jax.experimental.pallas import tpu as pltpu
from jax.sharding import PartitionSpec as P

ATTENTION_HEADS = 16
HEAD_SIZE = 48
SEG = 1024
RATE = 16
NEGATIVE_FLOOR = -1e30
LOG2_SCALE = 1.4426950408889634 / HEAD_SIZE**0.5
PAD = 16
LANES = 128
MESH = pl.DeviceIdType.MESH
BF16 = jnp.bfloat16
F32 = jnp.float32
VMEM = pl.BlockSpec(memory_space=pltpu.VMEM)
SMEM = pl.BlockSpec(memory_space=pltpu.SMEM)


def dot(a, b, ca=1, cb=0):
    return lax.dot_general(a, b, (((ca,), (cb,)), ((), ())), preferred_element_type=F32)


def head_rows(head):
    return pl.ds(pl.multiple_of(head * HEAD_SIZE, PAD), HEAD_SIZE)


def scaled_query(query):
    scaled = query.astype(F32) * LOG2_SCALE
    high = scaled.astype(BF16)
    low = (scaled - high.astype(F32)).astype(BF16)
    return jnp.concatenate([high, low, jnp.ones((PAD, query.shape[1]), BF16)], 0)


def masked_key(key, dead):
    row = lax.broadcasted_iota(jnp.int32, (PAD, key.shape[1]), 0)
    mask = jnp.where(dead & (row == 0), NEGATIVE_FLOOR, 0.0).astype(BF16)
    return jnp.concatenate([key, key, mask], 0)


def counted_value(value):
    return jnp.concatenate([value, jnp.ones((PAD, value.shape[1]), BF16)], 0)


def lanes(width):
    return lax.broadcasted_iota(jnp.int32, (PAD, width), 1)


def selector(length, offset):
    shape = (length, length // RATE)
    token = lax.broadcasted_iota(jnp.int32, shape, 0)
    pick = lax.broadcasted_iota(jnp.int32, shape, 1)
    return jnp.where(token == RATE * pick + offset, 1.0, 0.0).astype(BF16)


def project_kernel(offsets, x, wq, wk, wv, q_out, k_out, v_out, sel_out):
    length = x.shape[0]
    picked = length // RATE
    tiles = x[...]
    for weight, out in ((wk, k_out), (wv, v_out), (wq, q_out)):
        out[...] = dot(weight[...].T, tiles, 1, 1).astype(BF16)

    def pick(head, carry):
        rows = head_rows(head)
        onehot = selector(length, offsets[head])
        both = jnp.concatenate([k_out[rows, :], v_out[rows, :]], 0)
        chosen = dot(both, onehot).astype(BF16)
        sel_out[rows, :picked] = chosen[:HEAD_SIZE]
        sel_out[rows, picked:] = chosen[HEAD_SIZE:]
        return carry

    lax.fori_loop(0, ATTENTION_HEADS, pick, 0, unroll=4)


def local_kernel(base, live, q, k, v, out):
    length = q.shape[1]
    chunk = length // 2
    parts = 4
    step = length // parts
    dead = lanes(length) + base[0] >= live[0]

    def one_head(head, carry):
        rows = head_rows(head)
        query = scaled_query(q[rows, :])
        key = masked_key(k[rows, :], dead).T
        value = counted_value(v[rows, :])
        scores = dot(key, query[:, :chunk])
        for index in range(length // chunk):
            here = scores
            if (index + 1) * chunk < length:
                scores = dot(key, query[:, (index + 1) * chunk : (index + 2) * chunk])
            peak = jnp.max(here, axis=0, keepdims=True)
            total = None
            for part in range(parts):
                cut = slice(part * step, (part + 1) * step)
                weights = jnp.exp2(here[cut] - peak).astype(BF16)
                piece = dot(value[:, cut], weights)
                total = piece if total is None else total + piece
            done = total[:HEAD_SIZE] / total[HEAD_SIZE : HEAD_SIZE + 1]
            out[rows, index * chunk : (index + 1) * chunk] = done.astype(BF16)
        return carry

    lax.fori_loop(0, ATTENTION_HEADS, one_head, 0)


def dilated_kernel(base, live, offsets, q, k, v, gathered, near, w_out, cot, branch, grad, attn):
    length = q.shape[1]
    picked = length // RATE
    shards = gathered.shape[0]
    width = 2 * picked
    position = lanes(length) + base[0]
    dead = position >= live[0]
    slot = lanes(shards * width)
    inside = slot % width
    key_position = slot // width * length + inside * RATE

    def attend(key, query, value):
        scores = dot(key, query, 0, 0)
        peak = jnp.max(scores, axis=0, keepdims=True)
        weights = jnp.exp2(scores - peak).astype(BF16)
        return peak, dot(value, weights)

    def one_head(head, carry):
        rows = head_rows(head)
        offset = offsets[head]
        onehot = selector(length, offset)
        query = dot(scaled_query(q[rows, :]), onehot).astype(BF16)
        local_max, local_sum = attend(masked_key(k[rows, :], dead), query, counted_value(v[rows, :]))
        both = jnp.concatenate([gathered[shard, rows, :] for shard in range(shards)], 1)
        key_dead = (inside >= picked) | (key_position + offset >= live[0])
        value = jnp.concatenate([both[:, picked:], both[:, :picked]], 1)
        far_max, far_sum = attend(masked_key(both, key_dead), query, counted_value(value))
        top = jnp.maximum(local_max, far_max)
        total = jnp.exp2(local_max - top) * local_sum + jnp.exp2(far_max - top) * far_sum
        chosen = (total[:HEAD_SIZE] / total[HEAD_SIZE : HEAD_SIZE + 1]).astype(BF16)
        spread = dot(chosen, onehot, 1, 1)
        is_picked = position[:1] % RATE == offset
        merged = jnp.where(is_picked, spread, near[rows, :].astype(F32))
        attn[rows, :] = jnp.where(dead[:1], 0.0, merged).astype(BF16)
        return carry

    lax.fori_loop(0, ATTENTION_HEADS, one_head, 0, unroll=2)
    grad[...] = dot(attn[...], cot[...]).astype(BF16).T
    branch[...] = dot(attn[...].T, w_out[...]).astype(BF16)


def reduce_kernel(shards, slides, grad, out, stage, pair_in, chip, slide_in, chip_sum, line_in, final, *sems):
    pair_send, pair_recv, slide_send, slide_recv, line_send, line_recv, last_send, last_recv = sems
    me = lax.axis_index("seq")
    slide = lax.axis_index("dp")
    spots = shards // 2
    spot, core = me // 2, me % 2
    block = grad.shape[0] // shards
    tiles = grad.shape[1] // LANES
    part = block * tiles // slides
    ahead = [lax.rem(spot + k, spots) for k in range(spots)]
    others = [lax.rem(slide + k, slides) for k in range(slides)]
    partner = {"seq": me + 1 - 2 * core}

    barrier = pltpu.get_barrier_semaphore()
    peers = [partner]
    peers += [{"dp": others[k]} for k in range(1, slides)]
    peers += [{"seq": 2 * ahead[k] + core} for k in range(1, spots)]
    for peer in peers:
        pl.semaphore_signal(barrier, inc=1, device_id=peer, device_id_type=MESH)
    for shard in range(shards):
        for tile in range(tiles):
            stage[shard % 2, shard // 2, tile * block : (tile + 1) * block, :] = grad[
                shard * block : (shard + 1) * block, tile * LANES : (tile + 1) * LANES
            ]
    pl.semaphore_wait(barrier, len(peers))

    def copy(src, dst, send, recv, peer):
        item = pltpu.make_async_remote_copy(
            src_ref=src, dst_ref=dst, send_sem=send, recv_sem=recv, device_id=peer, device_id_type=MESH
        )
        item.start()
        return item

    turns = list(range(1, spots)) + [0]
    pair = {
        k: copy(stage.at[1 - core, ahead[k]], pair_in.at[k], pair_send.at[k], pair_recv.at[k], partner)
        for k in turns
    }
    across = {}
    for k in turns:
        pair[k].wait_recv()
        for p in range(slides):
            rows = slice(p * part, (p + 1) * part)
            mine = stage[core, ahead[k], rows, :].astype(F32) + pair_in[k, rows, :].astype(F32)
            chip[k, p] = mine.astype(BF16)
        for j in range(1, slides):
            across[k, j] = copy(
                chip.at[k, others[j]],
                slide_in.at[k, j - 1],
                slide_send.at[k, j - 1],
                slide_recv.at[k, j - 1],
                {"dp": others[j]},
            )
    along = {}
    for k in turns:
        total = chip[k, slide].astype(F32)
        for j in range(1, slides):
            across[k, j].wait_recv()
            total = total + slide_in[k, j - 1].astype(F32)
        chip_sum[k] = total.astype(BF16)
        if k:
            along[k] = copy(
                chip_sum.at[k],
                line_in.at[k - 1],
                line_send.at[k - 1],
                line_recv.at[k - 1],
                {"seq": 2 * ahead[k] + core},
            )
    total = chip_sum[0].astype(F32)
    for k in range(1, spots):
        along[k].wait_recv()
        total = total + line_in[k - 1].astype(F32)
    own = pl.ds(pl.multiple_of(slide * part, PAD), part)
    final[own, :] = total.astype(BF16)
    last = [
        copy(final.at[own, :], final.at[own, :], last_send.at[j - 1], last_recv.at[j - 1], {"dp": others[j]})
        for j in range(1, slides)
    ]
    for item in last:
        item.wait_recv()
    for item in list(pair.values()) + list(across.values()) + list(along.values()) + last:
        item.wait_send()
    for tile in range(tiles):
        out[tile * LANES : (tile + 1) * LANES, :] = final[tile * block : (tile + 1) * block, :].astype(F32).T


def reduce_gradient(grad, shards, slides):
    width = grad.shape[0]
    block = width // shards
    rows = block * (grad.shape[1] // LANES)
    if block % PAD or rows % (slides * PAD) or shards % 2 or shards < 4 or slides < 2:
        share = lax.psum_scatter(grad, "seq", scatter_dimension=0, tiled=True)
        return lax.psum(share, "dp").astype(F32).T
    spots = shards // 2
    part = rows // slides
    dma = pltpu.SemaphoreType.DMA
    return pl.pallas_call(
        functools.partial(reduce_kernel, shards, slides),
        out_shape=jax.ShapeDtypeStruct((grad.shape[1], block), F32),
        in_specs=[VMEM],
        out_specs=VMEM,
        scratch_shapes=[
            pltpu.VMEM((2, spots, rows, LANES), BF16),
            pltpu.VMEM((spots, rows, LANES), BF16),
            pltpu.VMEM((spots, slides, part, LANES), BF16),
            pltpu.VMEM((spots, slides - 1, part, LANES), BF16),
            pltpu.VMEM((spots, part, LANES), BF16),
            pltpu.VMEM((spots - 1, part, LANES), BF16),
            pltpu.VMEM((rows, LANES), BF16),
            dma((spots,)),
            dma((spots,)),
            dma((spots, slides - 1)),
            dma((spots, slides - 1)),
            dma((spots - 1,)),
            dma((spots - 1,)),
            dma((slides - 1,)),
            dma((slides - 1,)),
        ],
        compiler_params=pltpu.CompilerParams(
            vmem_limit_bytes=60 << 20, collective_id=0, has_side_effects=True
        ),
    )(grad)


def params():
    return pltpu.CompilerParams(vmem_limit_bytes=60 << 20)


def body(shards, slides, tiles, tile_count, offsets, w_query, w_key, w_value, w_out, cotangent):
    inputs = tiles[0]
    length, width = inputs.shape
    assert length == SEG
    picked = length // RATE
    base = (lax.axis_index("seq") * length).astype(jnp.int32).reshape(1)
    half = jax.ShapeDtypeStruct((width, length), BF16)
    query, key, value, chosen = pl.pallas_call(
        project_kernel,
        out_shape=(half, half, half, jax.ShapeDtypeStruct((width, 2 * picked), BF16)),
        in_specs=[SMEM] + [VMEM] * 4,
        out_specs=(VMEM,) * 4,
        compiler_params=params(),
    )(offsets, inputs, w_query, w_key, w_value)
    gathered = lax.all_gather(chosen, "seq", axis=0)
    near = pl.pallas_call(
        local_kernel,
        out_shape=half,
        in_specs=[SMEM] * 2 + [VMEM] * 3,
        out_specs=VMEM,
        compiler_params=params(),
        cost_estimate=pl.CostEstimate(flops=2 * 10**10, bytes_accessed=6 * 10**6, transcendentals=2 * 10**7),
    )(base, tile_count, query, key, value)
    branch, grad = pl.pallas_call(
        dilated_kernel,
        out_shape=(
            jax.ShapeDtypeStruct((length, width), BF16),
            jax.ShapeDtypeStruct((width, width), BF16),
        ),
        in_specs=[SMEM] * 3 + [VMEM] * 7,
        out_specs=(VMEM,) * 2,
        scratch_shapes=[pltpu.VMEM((width, length), BF16)],
        compiler_params=params(),
    )(base, tile_count, offsets, query, key, value, gathered, near, w_out, cotangent[0])
    return (branch[None], reduce_gradient(grad, shards, slides))


def solution(mesh):
    in_specs = (P("dp", "seq", None), P("dp"), P(), P(), P(), P(), P(), P("dp", "seq", None))
    out_specs = (P("dp", "seq", None), P(None, "seq"))
    run = functools.partial(body, mesh.shape["seq"], mesh.shape["dp"])
    return jax.shard_map(run, mesh=mesh, in_specs=in_specs, out_specs=out_specs, check_vma=False)
```

```python
import functools

import jax
import jax.numpy as jnp
from jax import lax
from jax.experimental import pallas as pl
from jax.experimental.pallas import tpu as pltpu
from jax.sharding import PartitionSpec as P

ATTENTION_HEADS = 16
HEAD_SIZE = 48
SEG = 1024
RATE = 16
NEGATIVE_FLOOR = -1e30
LOG2_SCALE = 1.4426950408889634 / HEAD_SIZE**0.5
PAD = 16
LANES = 128
MESH = pl.DeviceIdType.MESH
BF16 = jnp.bfloat16
F32 = jnp.float32
VMEM = pl.BlockSpec(memory_space=pltpu.VMEM)
SMEM = pl.BlockSpec(memory_space=pltpu.SMEM)


def dot(a, b, ca=1, cb=0):
    return lax.dot_general(a, b, (((ca,), (cb,)), ((), ())), preferred_element_type=F32)


def head_rows(head):
    return pl.ds(pl.multiple_of(head * HEAD_SIZE, PAD), HEAD_SIZE)


def scaled_query(query):
    scaled = query.astype(F32) * LOG2_SCALE
    high = scaled.astype(BF16)
    low = (scaled - high.astype(F32)).astype(BF16)
    return jnp.concatenate([high, low, jnp.ones((PAD, query.shape[1]), BF16)], 0)


def masked_key(key, dead):
    row = lax.broadcasted_iota(jnp.int32, (PAD, key.shape[1]), 0)
    mask = jnp.where(dead & (row == 0), NEGATIVE_FLOOR, 0.0).astype(BF16)
    return jnp.concatenate([key, key, mask], 0)


def counted_value(value):
    return jnp.concatenate([value, jnp.ones((PAD, value.shape[1]), BF16)], 0)


def lanes(width):
    return lax.broadcasted_iota(jnp.int32, (PAD, width), 1)


def selector(length, offset):
    shape = (length, length // RATE)
    token = lax.broadcasted_iota(jnp.int32, shape, 0)
    pick = lax.broadcasted_iota(jnp.int32, shape, 1)
    return jnp.where(token == RATE * pick + offset, 1.0, 0.0).astype(BF16)


def attention_kernel(
    shards, slides, fused, live, offsets, x, wq, wk, wv, w_out, cot, branch, grad, q, k, v, near, attn, chosen,
    gathered, gather_send, gather_recv, *scratch
):
    width, length = q.shape
    picked = length // RATE
    block = 2 * picked
    half = ATTENTION_HEADS // 2
    me = lax.axis_index("seq")
    slide = lax.axis_index("dp")
    spots = shards // 2
    spot, core = me // 2, me % 2
    ahead = [lax.rem(spot + n, spots) for n in range(spots)]
    others = [lax.rem(slide + n, slides) for n in range(slides)]
    partner = {"seq": me + 1 - 2 * core}
    line = [{"seq": 2 * ahead[n] + core} for n in range(spots)]
    peers = [partner] + line[1:]
    if fused:
        peers = peers + [{"dp": others[n]} for n in range(1, slides)]
    barrier = pltpu.get_barrier_semaphore()
    for peer in peers:
        pl.semaphore_signal(barrier, inc=1, device_id=peer, device_id_type=MESH)

    def copy(src, dst, send, recv, peer):
        item = pltpu.make_async_remote_copy(
            src_ref=src, dst_ref=dst, send_sem=send, recv_sem=recv, device_id=peer, device_id_type=MESH
        )
        item.start()
        return item

    tiles = x[...]
    for weight, out in ((wk, k), (wv, v)):
        out[...] = dot(weight[...].T, tiles, 1, 1).astype(BF16)

    def pick(head, carry):
        rows = head_rows(head)
        onehot = selector(length, offsets[head])
        both = jnp.concatenate([k[rows, :], v[rows, :]], 0)
        part = dot(both, onehot).astype(BF16)
        chosen[rows, :picked] = part[:HEAD_SIZE]
        chosen[rows, picked:] = part[HEAD_SIZE:]
        return carry

    lax.fori_loop(0, ATTENTION_HEADS, pick, 0, unroll=4)
    pl.semaphore_wait(barrier, len(peers))
    pending = []
    for n in range(1, spots):
        pending.append(copy(chosen, gathered.at[0, n], gather_send.at[0, n], gather_recv.at[0, n], line[n]))
    pending.append(copy(chosen, gathered.at[1, 0], gather_send.at[1, 0], gather_recv.at[1, 0], partner))
    gathered[0, 0] = chosen[...]
    q[...] = dot(wq[...].T, tiles, 1, 1).astype(BF16)

    position = lanes(length) + me * length
    dead = position >= live[0]
    inside = lanes(block)

    def local(head):
        chunk = length // 2
        parts = 4
        step = length // parts
        rows = head_rows(head)
        query = scaled_query(q[rows, :])
        key = masked_key(k[rows, :], dead).T
        value = counted_value(v[rows, :])
        scores = dot(key, query[:, :chunk])
        for index in range(length // chunk):
            here = scores
            if (index + 1) * chunk < length:
                scores = dot(key, query[:, (index + 1) * chunk : (index + 2) * chunk])
            peak = jnp.max(here, axis=0, keepdims=True)
            total = None
            for part in range(parts):
                cut = slice(part * step, (part + 1) * step)
                weights = jnp.exp2(here[cut] - peak).astype(BF16)
                piece = dot(value[:, cut], weights)
                total = piece if total is None else total + piece
            done = total[:HEAD_SIZE] / total[HEAD_SIZE : HEAD_SIZE + 1]
            near[rows, index * chunk : (index + 1) * chunk] = done.astype(BF16)

    def attend(key, query, value):
        scores = dot(key, query, 0, 0)
        peak = jnp.max(scores, axis=0, keepdims=True)
        weights = jnp.exp2(scores - peak).astype(BF16)
        return peak, dot(value, weights)

    def dilated(head):
        rows = head_rows(head)
        offset = offsets[head]
        onehot = selector(length, offset)
        query = dot(scaled_query(q[rows, :]), onehot).astype(BF16)
        local_max, local_sum = attend(masked_key(k[rows, :], dead), query, counted_value(v[rows, :]))
        keys, gone = [], []
        for side in range(2):
            for n in range(spots):
                keys.append(gathered[side, n, rows, :])
                origin = 2 * lax.rem(spot - n + spots, spots) + lax.rem(core + side, 2)
                gone.append((inside >= picked) | (origin * length + inside * RATE + offset >= live[0]))
        both = jnp.concatenate(keys, 1)
        gone = jnp.concatenate([jnp.where(item, 1, 0) for item in gone], 1) == 1
        value = jnp.concatenate([both[:, picked:], both[:, :picked]], 1)
        far_max, far_sum = attend(masked_key(both, gone), query, counted_value(value))
        top = jnp.maximum(local_max, far_max)
        total = jnp.exp2(local_max - top) * local_sum + jnp.exp2(far_max - top) * far_sum
        part = (total[:HEAD_SIZE] / total[HEAD_SIZE : HEAD_SIZE + 1]).astype(BF16)
        spread = dot(part, onehot, 1, 1)
        is_picked = position[:1] % RATE == offset
        merged = jnp.where(is_picked, spread, near[rows, :].astype(F32))
        attn[rows, :] = jnp.where(dead[:1], 0.0, merged).astype(BF16)

    def first(head, carry):
        local(head)
        return carry

    def second(head, carry):
        dilated(head)
        local(head + half)
        return carry

    def third(pair, carry):
        dilated(2 * pair)
        dilated(2 * pair + 1)
        return carry

    lax.fori_loop(0, half, first, 0)
    for n in range(1, spots):
        pending[n - 1].wait_recv()
        pending.append(
            copy(gathered.at[0, n], gathered.at[1, n], gather_send.at[1, n], gather_recv.at[1, n], partner)
        )
    for item in pending[spots - 1 :]:
        item.wait_recv()
    lax.fori_loop(0, half, second, 0)

    def gradient(rows):
        return dot(attn[rows, :], cot[...]).astype(BF16).T

    if not fused:
        lax.fori_loop(half // 2, half, third, 0)
        grad[...] = gradient(slice(0, width))
        branch[...] = dot(attn[...].T, w_out[...]).astype(BF16)
        for item in pending:
            item.wait_send()
        return

    stage, pair_in, chip, slide_in, chip_sum, line_in, final = scratch[:7]
    pair_send, pair_recv, slide_send, slide_recv, line_send, line_recv, last_send, last_recv = scratch[7:]
    columns = width // shards
    wide = width // 2
    count = wide // LANES
    part = columns * count // slides
    turns = list(range(1, spots)) + [0]
    pair, across, along, last = {}, {}, {}, {}

    def open_pair(g):
        share = gradient(slice(g * wide, (g + 1) * wide))
        for shard in range(shards):
            for tile in range(count):
                stage[g, shard % 2, shard // 2, tile * columns : (tile + 1) * columns, :] = share[
                    shard * columns : (shard + 1) * columns, tile * LANES : (tile + 1) * LANES
                ]
        for n in turns:
            pair[g, n] = copy(
                stage.at[g, 1 - core, ahead[n]],
                pair_in.at[g, n],
                pair_send.at[g, n],
                pair_recv.at[g, n],
                partner,
            )

    def open_across(g):
        for n in turns:
            pair[g, n].wait_recv()
            mine = stage[g, core, ahead[n]].astype(F32) + pair_in[g, n].astype(F32)
            for p in range(slides):
                chip[g, n, p] = mine[p * part : (p + 1) * part].astype(BF16)
            for j in range(1, slides):
                across[g, n, j] = copy(
                    chip.at[g, n, others[j]],
                    slide_in.at[g, n, j - 1],
                    slide_send.at[g, n, j - 1],
                    slide_recv.at[g, n, j - 1],
                    {"dp": others[j]},
                )

    def open_along(g):
        for n in turns:
            total = chip[g, n, slide].astype(F32)
            for j in range(1, slides):
                across[g, n, j].wait_recv()
                total = total + slide_in[g, n, j - 1].astype(F32)
            chip_sum[g, n] = total.astype(BF16)
            if n:
                along[g, n] = copy(
                    chip_sum.at[g, n],
                    line_in.at[g, n - 1],
                    line_send.at[g, n - 1],
                    line_recv.at[g, n - 1],
                    line[n],
                )

    def open_last(g):
        total = chip_sum[g, 0].astype(F32)
        for n in range(1, spots):
            along[g, n].wait_recv()
            total = total + line_in[g, n - 1].astype(F32)
        final[g, slide] = total.astype(BF16)
        for j in range(1, slides):
            last[g, j] = copy(
                final.at[g, slide],
                final.at[g, slide],
                last_send.at[g, j - 1],
                last_recv.at[g, j - 1],
                {"dp": others[j]},
            )

    def close(g):
        for j in range(1, slides):
            last[g, j].wait_recv()
        full = jnp.concatenate([final[g, p].astype(F32) for p in range(slides)], 0)
        for tile in range(count):
            rows = slice(g * wide + tile * LANES, g * wide + (tile + 1) * LANES)
            grad[rows, :] = full[tile * columns : (tile + 1) * columns].T

    open_pair(0)
    lax.fori_loop(half // 2, half // 2 + half // 4, third, 0)
    open_across(0)
    lax.fori_loop(half // 2 + half // 4, half, third, 0)
    open_along(0)
    open_pair(1)
    open_last(0)
    open_across(1)
    branch[...] = dot(attn[...].T, w_out[...]).astype(BF16)
    open_along(1)
    close(0)
    open_last(1)
    close(1)
    for group in (pending, pair.values(), across.values(), along.values(), last.values()):
        for item in group:
            item.wait_send()


def body(shards, slides, tiles, tile_count, offsets, w_query, w_key, w_value, w_out, cotangent):
    inputs = tiles[0]
    length, width = inputs.shape
    assert length == SEG and shards % 2 == 0
    spots = shards // 2
    columns = width // shards
    rows = columns * (width // 2 // LANES)
    fused = columns % PAD == 0 and rows % (8 * slides) == 0 and spots > 1 and slides > 1
    dma = pltpu.SemaphoreType.DMA
    held = pltpu.VMEM((width, length), BF16)
    block = 2 * (length // RATE)
    scratch = [held] * 5 + [
        pltpu.VMEM((width, block), BF16),
        pltpu.VMEM((2, spots, width, block), BF16),
        dma((2, spots)),
        dma((2, spots)),
    ]
    grad_type = jax.ShapeDtypeStruct((width, width), BF16)
    if fused:
        part = rows // slides
        grad_type = jax.ShapeDtypeStruct((width, columns), F32)
        scratch += [
            pltpu.VMEM((2, 2, spots, rows, LANES), BF16),
            pltpu.VMEM((2, spots, rows, LANES), BF16),
            pltpu.VMEM((2, spots, slides, part, LANES), BF16),
            pltpu.VMEM((2, spots, slides - 1, part, LANES), BF16),
            pltpu.VMEM((2, spots, part, LANES), BF16),
            pltpu.VMEM((2, spots - 1, part, LANES), BF16),
            pltpu.VMEM((2, slides, part, LANES), BF16),
        ]
        for shape in ((2, spots), (2, spots, slides - 1), (2, spots - 1), (2, slides - 1)):
            scratch += [dma(shape), dma(shape)]
    branch, grad = pl.pallas_call(
        functools.partial(attention_kernel, shards, slides, fused),
        out_shape=(jax.ShapeDtypeStruct((length, width), BF16), grad_type),
        in_specs=[SMEM] * 2 + [VMEM] * 6,
        out_specs=(VMEM,) * 2,
        scratch_shapes=scratch,
        compiler_params=pltpu.CompilerParams(
            vmem_limit_bytes=60 << 20, collective_id=0, has_side_effects=True
        ),
    )(tile_count, offsets, inputs, w_query, w_key, w_value, w_out, cotangent[0])
    if not fused:
        share = lax.psum_scatter(grad, "seq", scatter_dimension=0, tiled=True)
        grad = lax.psum(share, "dp").astype(F32).T
    return (branch[None], grad)


def solution(mesh):
    in_specs = (P("dp", "seq", None), P("dp"), P(), P(), P(), P(), P(), P("dp", "seq", None))
    out_specs = (P("dp", "seq", None), P(None, "seq"))
    run = functools.partial(body, mesh.shape["seq"], mesh.shape["dp"])
    return jax.shard_map(run, mesh=mesh, in_specs=in_specs, out_specs=out_specs, check_vma=False)
```

```python
import functools

import jax
import jax.numpy as jnp
from jax import lax
from jax.experimental import pallas as pl
from jax.experimental.pallas import tpu as pltpu
from jax.sharding import PartitionSpec as P

ATTENTION_HEADS = 16
HEAD_SIZE = 48
SEG = 1024
RATE = 16
NEGATIVE_FLOOR = -1e30
LOG2_SCALE = 1.4426950408889634 / HEAD_SIZE**0.5
PAD = 16
LANES = 128
MESH = pl.DeviceIdType.MESH
BF16 = jnp.bfloat16
F32 = jnp.float32
VMEM = pl.BlockSpec(memory_space=pltpu.VMEM)
SMEM = pl.BlockSpec(memory_space=pltpu.SMEM)


def dot(a, b, ca=1, cb=0):
    return lax.dot_general(a, b, (((ca,), (cb,)), ((), ())), preferred_element_type=F32)


def head_rows(head):
    return pl.ds(pl.multiple_of(head * HEAD_SIZE, PAD), HEAD_SIZE)


def scaled_query(query):
    scaled = query.astype(F32) * LOG2_SCALE
    high = scaled.astype(BF16)
    low = (scaled - high.astype(F32)).astype(BF16)
    return jnp.concatenate([high, low, jnp.ones((PAD, query.shape[1]), BF16)], 0)


def masked_key(key, dead):
    row = lax.broadcasted_iota(jnp.int32, (PAD, key.shape[1]), 0)
    mask = jnp.where(dead & (row == 0), NEGATIVE_FLOOR, 0.0).astype(BF16)
    return jnp.concatenate([key, key, mask], 0)


def counted_value(value):
    return jnp.concatenate([value, jnp.ones((PAD, value.shape[1]), BF16)], 0)


def lanes(width):
    return lax.broadcasted_iota(jnp.int32, (PAD, width), 1)


def selector(length, offset):
    shape = (length, length // RATE)
    token = lax.broadcasted_iota(jnp.int32, shape, 0)
    pick = lax.broadcasted_iota(jnp.int32, shape, 1)
    return jnp.where(token == RATE * pick + offset, 1.0, 0.0).astype(BF16)


def attention_kernel(
    shards, slides, fused, live, offsets, x, wq, wk, wv, w_out, cot, branch, grad, q, k, v, near, attn, chosen,
    gathered, gather_send, gather_recv, *scratch
):
    width, length = q.shape
    picked = length // RATE
    block = 2 * picked
    half = ATTENTION_HEADS // 2
    lead = half + 2
    me = lax.axis_index("seq")
    slide = lax.axis_index("dp")
    spots = shards // 2
    spot, core = me // 2, me % 2
    ahead = [lax.rem(spot + n, spots) for n in range(spots)]
    others = [lax.rem(slide + n, slides) for n in range(slides)]
    partner = {"seq": me + 1 - 2 * core}
    line = [{"seq": 2 * ahead[n] + core} for n in range(spots)]
    peers = [partner] + line[1:]
    if fused:
        peers = peers + [{"dp": others[n]} for n in range(1, slides)]
    barrier = pltpu.get_barrier_semaphore()
    for peer in peers:
        pl.semaphore_signal(barrier, inc=1, device_id=peer, device_id_type=MESH)

    def copy(src, dst, send, recv, peer):
        item = pltpu.make_async_remote_copy(
            src_ref=src, dst_ref=dst, send_sem=send, recv_sem=recv, device_id=peer, device_id_type=MESH
        )
        item.start()
        return item

    tiles = x[...]
    for weight, out in ((wk, k), (wv, v)):
        out[...] = dot(weight[...].T, tiles, 1, 1).astype(BF16)

    def pick(head, carry):
        rows = head_rows(head)
        onehot = selector(length, offsets[head])
        both = jnp.concatenate([k[rows, :], v[rows, :]], 0)
        part = dot(both, onehot).astype(BF16)
        chosen[rows, :picked] = part[:HEAD_SIZE]
        chosen[rows, picked:] = part[HEAD_SIZE:]
        return carry

    lax.fori_loop(0, ATTENTION_HEADS, pick, 0, unroll=4)
    pl.semaphore_wait(barrier, len(peers))
    def relay(src, origin, way):
        slot = gathered.at[1 if way == 2 else 0, origin]
        return pltpu.make_async_remote_copy(
            src_ref=src,
            dst_ref=slot,
            send_sem=gather_send.at[way, origin],
            recv_sem=gather_recv.at[1 if way == 2 else 0, origin],
            device_id=({"seq": me + 2}, {"seq": me - 2}, partner)[way],
            device_id_type=MESH,
        )

    @pl.when(spot < spots - 1)
    def _():
        relay(chosen, spot, 0).start()

    @pl.when(spot > 0)
    def _():
        relay(chosen, spot, 1).start()

    relay(chosen, spot, 2).start()
    gathered[0, spot] = chosen[...]

    def pass_on(step):
        @pl.when(spot >= step)
        def _():
            origin = spot - step
            slot = gathered.at[0, origin]
            relay(slot, origin, 0).wait_recv()

            @pl.when(spot < spots - 1)
            def _():
                relay(slot, origin, 0).start()

            relay(slot, origin, 2).start()

        @pl.when(spot + step < spots)
        def _():
            origin = spot + step
            slot = gathered.at[0, origin]
            relay(slot, origin, 1).wait_recv()

            @pl.when(spot > 0)
            def _():
                relay(slot, origin, 1).start()

            relay(slot, origin, 2).start()

    def end_gather():
        for origin in range(spots):
            slot = gathered.at[0, origin]

            @pl.when((spot >= origin) & (spot < spots - 1))
            def _():
                relay(slot, origin, 0).wait_send()

            @pl.when((spot <= origin) & (spot > 0))
            def _():
                relay(slot, origin, 1).wait_send()

            relay(slot, origin, 2).wait_send()

    q[...] = dot(wq[...].T, tiles, 1, 1).astype(BF16)

    position = lanes(length) + me * length
    dead = position >= live[0]
    inside = lanes(block)

    def local(head):
        chunk = length // 2
        parts = 4
        step = length // parts
        rows = head_rows(head)
        query = scaled_query(q[rows, :])
        key = masked_key(k[rows, :], dead).T
        value = counted_value(v[rows, :])
        scores = dot(key, query[:, :chunk])
        for index in range(length // chunk):
            here = scores
            if (index + 1) * chunk < length:
                scores = dot(key, query[:, (index + 1) * chunk : (index + 2) * chunk])
            peak = jnp.max(here, axis=0, keepdims=True)
            total = None
            for part in range(parts):
                cut = slice(part * step, (part + 1) * step)
                weights = jnp.exp2(here[cut] - peak).astype(BF16)
                piece = dot(value[:, cut], weights)
                total = piece if total is None else total + piece
            done = total[:HEAD_SIZE] / total[HEAD_SIZE : HEAD_SIZE + 1]
            near[rows, index * chunk : (index + 1) * chunk] = done.astype(BF16)

    def attend(key, query, value):
        scores = dot(key, query, 0, 0)
        peak = jnp.max(scores, axis=0, keepdims=True)
        weights = jnp.exp2(scores - peak).astype(BF16)
        return peak, dot(value, weights)

    def dilated(head):
        rows = head_rows(head)
        offset = offsets[head]
        onehot = selector(length, offset)
        query = dot(scaled_query(q[rows, :]), onehot).astype(BF16)
        local_max, local_sum = attend(masked_key(k[rows, :], dead), query, counted_value(v[rows, :]))
        keys, gone = [], []
        for side in range(2):
            for n in range(spots):
                keys.append(gathered[side, n, rows, :])
                origin = 2 * n + lax.rem(core + side, 2)
                gone.append((inside >= picked) | (origin * length + inside * RATE + offset >= live[0]))
        both = jnp.concatenate(keys, 1)
        gone = jnp.concatenate([jnp.where(item, 1, 0) for item in gone], 1) == 1
        value = jnp.concatenate([both[:, picked:], both[:, :picked]], 1)
        far_max, far_sum = attend(masked_key(both, gone), query, counted_value(value))
        top = jnp.maximum(local_max, far_max)
        total = jnp.exp2(local_max - top) * local_sum + jnp.exp2(far_max - top) * far_sum
        part = (total[:HEAD_SIZE] / total[HEAD_SIZE : HEAD_SIZE + 1]).astype(BF16)
        spread = dot(part, onehot, 1, 1)
        is_picked = position[:1] % RATE == offset
        merged = jnp.where(is_picked, spread, near[rows, :].astype(F32))
        attn[rows, :] = jnp.where(dead[:1], 0.0, merged).astype(BF16)

    def first(head, carry):
        local(head)
        return carry

    def second(head, carry):
        dilated(head)
        local(head + lead)
        return carry

    def third(pair, carry):
        dilated(2 * pair)
        dilated(2 * pair + 1)
        return carry

    cuts = [n * (lead - 1) // (spots - 1) for n in range(spots)]
    for step in range(1, spots):
        lax.fori_loop(cuts[step - 1], cuts[step], first, 0)
        pass_on(step)
    lax.fori_loop(cuts[-1], lead, first, 0)
    for origin in range(spots):
        relay(gathered.at[0, origin], origin, 2).wait_recv()
    lax.fori_loop(0, ATTENTION_HEADS - lead, second, 0)
    lax.fori_loop((ATTENTION_HEADS - lead) // 2, half // 2, third, 0)

    def gradient(rows):
        return dot(attn[rows, :], cot[...]).astype(BF16).T

    if not fused:
        lax.fori_loop(half // 2, half, third, 0)
        grad[...] = gradient(slice(0, width))
        branch[...] = dot(attn[...].T, w_out[...]).astype(BF16)
        end_gather()
        return

    stage, pair_in, chip, slide_in, chip_sum, line_in, final = scratch[:7]
    pair_send, pair_recv, slide_send, slide_recv, line_send, line_recv, last_send, last_recv = scratch[7:]
    columns = width // shards
    wide = width // 2
    count = wide // LANES
    part = columns * count // slides
    turns = list(range(1, spots)) + [0]
    pair, across, along, last = {}, {}, {}, {}

    def open_pair(g):
        share = gradient(slice(g * wide, (g + 1) * wide))
        for shard in range(shards):
            for tile in range(count):
                stage[g, shard % 2, shard // 2, tile * columns : (tile + 1) * columns, :] = share[
                    shard * columns : (shard + 1) * columns, tile * LANES : (tile + 1) * LANES
                ]
        for n in turns:
            pair[g, n] = copy(
                stage.at[g, 1 - core, ahead[n]],
                pair_in.at[g, n],
                pair_send.at[g, n],
                pair_recv.at[g, n],
                partner,
            )

    def open_across(g):
        for n in turns:
            pair[g, n].wait_recv()
            mine = stage[g, core, ahead[n]].astype(F32) + pair_in[g, n].astype(F32)
            for p in range(slides):
                chip[g, n, p] = mine[p * part : (p + 1) * part].astype(BF16)
            for j in range(1, slides):
                across[g, n, j] = copy(
                    chip.at[g, n, others[j]],
                    slide_in.at[g, n, j - 1],
                    slide_send.at[g, n, j - 1],
                    slide_recv.at[g, n, j - 1],
                    {"dp": others[j]},
                )

    def open_along(g):
        for n in turns:
            total = chip[g, n, slide].astype(F32)
            for j in range(1, slides):
                across[g, n, j].wait_recv()
                total = total + slide_in[g, n, j - 1].astype(F32)
            chip_sum[g, n] = total.astype(BF16)
            if n:
                along[g, n] = copy(
                    chip_sum.at[g, n],
                    line_in.at[g, n - 1],
                    line_send.at[g, n - 1],
                    line_recv.at[g, n - 1],
                    line[n],
                )

    def open_last(g):
        total = chip_sum[g, 0].astype(F32)
        for n in range(1, spots):
            along[g, n].wait_recv()
            total = total + line_in[g, n - 1].astype(F32)
        final[g, slide] = total.astype(BF16)
        for j in range(1, slides):
            last[g, j] = copy(
                final.at[g, slide],
                final.at[g, slide],
                last_send.at[g, j - 1],
                last_recv.at[g, j - 1],
                {"dp": others[j]},
            )

    def close(g):
        for j in range(1, slides):
            last[g, j].wait_recv()
        full = jnp.concatenate([final[g, p].astype(F32) for p in range(slides)], 0)
        for tile in range(count):
            rows = slice(g * wide + tile * LANES, g * wide + (tile + 1) * LANES)
            grad[rows, :] = full[tile * columns : (tile + 1) * columns].T

    open_pair(0)
    lax.fori_loop(half // 2, half // 2 + half // 4, third, 0)
    open_across(0)
    lax.fori_loop(half // 2 + half // 4, half, third, 0)
    open_along(0)
    open_pair(1)
    open_last(0)
    open_across(1)
    branch[...] = dot(attn[...].T, w_out[...]).astype(BF16)
    open_along(1)
    close(0)
    open_last(1)
    close(1)
    end_gather()
    for group in (pair.values(), across.values(), along.values(), last.values()):
        for item in group:
            item.wait_send()


def body(shards, slides, tiles, tile_count, offsets, w_query, w_key, w_value, w_out, cotangent):
    inputs = tiles[0]
    length, width = inputs.shape
    assert length == SEG and shards % 2 == 0
    spots = shards // 2
    columns = width // shards
    rows = columns * (width // 2 // LANES)
    fused = columns % PAD == 0 and rows % (8 * slides) == 0 and spots > 1 and slides > 1
    dma = pltpu.SemaphoreType.DMA
    held = pltpu.VMEM((width, length), BF16)
    block = 2 * (length // RATE)
    scratch = [held] * 5 + [
        pltpu.VMEM((width, block), BF16),
        pltpu.VMEM((2, spots, width, block), BF16),
        dma((3, spots)),
        dma((2, spots)),
    ]
    grad_type = jax.ShapeDtypeStruct((width, width), BF16)
    if fused:
        part = rows // slides
        grad_type = jax.ShapeDtypeStruct((width, columns), F32)
        scratch += [
            pltpu.VMEM((2, 2, spots, rows, LANES), BF16),
            pltpu.VMEM((2, spots, rows, LANES), BF16),
            pltpu.VMEM((2, spots, slides, part, LANES), BF16),
            pltpu.VMEM((2, spots, slides - 1, part, LANES), BF16),
            pltpu.VMEM((2, spots, part, LANES), BF16),
            pltpu.VMEM((2, spots - 1, part, LANES), BF16),
            pltpu.VMEM((2, slides, part, LANES), BF16),
        ]
        for shape in ((2, spots), (2, spots, slides - 1), (2, spots - 1), (2, slides - 1)):
            scratch += [dma(shape), dma(shape)]
    branch, grad = pl.pallas_call(
        functools.partial(attention_kernel, shards, slides, fused),
        out_shape=(jax.ShapeDtypeStruct((length, width), BF16), grad_type),
        in_specs=[SMEM] * 2 + [VMEM] * 6,
        out_specs=(VMEM,) * 2,
        scratch_shapes=scratch,
        compiler_params=pltpu.CompilerParams(
            vmem_limit_bytes=60 << 20, collective_id=0, has_side_effects=True
        ),
    )(tile_count, offsets, inputs, w_query, w_key, w_value, w_out, cotangent[0])
    if not fused:
        share = lax.psum_scatter(grad, "seq", scatter_dimension=0, tiled=True)
        grad = lax.psum(share, "dp").astype(F32).T
    return (branch[None], grad)


def solution(mesh):
    in_specs = (P("dp", "seq", None), P("dp"), P(), P(), P(), P(), P(), P("dp", "seq", None))
    out_specs = (P("dp", "seq", None), P(None, "seq"))
    run = functools.partial(body, mesh.shape["seq"], mesh.shape["dp"])
    return jax.shard_map(run, mesh=mesh, in_specs=in_specs, out_specs=out_specs, check_vma=False)
```
